256 devices in a mesh: depth: 16 (over x_lo, z), tok: 16 (over x_hi, y, core).
Axes of the slice: x: 4 (x_hi: 2, x_lo: 2; x = x_hi * 2 + x_lo), y: 4, z: 8, core: 2. Of those that a mesh axis runs over, the one named last changes fastest.
Arguments:
- states: bfloat16 [16, 16384, 2048], P('depth', 'tok'), may hold values from -40 to 40
- w_query: bfloat16 [2048, 1024], replicated, may hold values from -0.25 to 0.25
- w_key: bfloat16 [2048, 256], replicated, may hold values from -0.25 to 0.25
- w_value: bfloat16 [2048, 256], replicated, may hold values from -0.125 to 0.125
Outputs:
- window_out: bfloat16 [16, 16384, 1024], P('depth', 'tok')
- depth_out: bfloat16 [16384, 1024], P(('tok', 'depth'))
The draws below stay inside these ranges and needn't reach their ends.
All inputs are finite; a program needn't handle non-finite values.
Results may differ from the reference program's by a relative error of at most 0.012.
The reference program's roundings to bfloat16 on the way count: a program that leaves them out, or rounds other values in their place, can miss the bound.
Values may be sent and summed in bfloat16 or wider, within the bound.
A program may use at most 192 MiB of HBM per device.

```python
import jax
import jax.numpy as jnp
from jax import lax

D = 2048
HQ = 8
HK = 2
HD = 128
WINDOW = 256
TOK_DEV = 1024
STEPS = 16
QW = 1024
KW = 256
TOKENS = 16384


def make_weights(key):
    base = jax.random.fold_in(key, 11)
    w_first = jax.random.normal(jax.random.fold_in(base, 1), (D, QW), jnp.float32) * D ** (-0.5)
    noise = jax.random.normal(jax.random.fold_in(base, 2), (D, KW), jnp.float32) * D ** (-0.5)
    w_second = noise
    return (jnp.clip(w_first, -0.25, 0.25), jnp.clip(w_second, -0.25, 0.25))


def draw_w_query(key, part):
    return make_weights(key)[0].astype(jnp.bfloat16)


def draw_w_key(key, part):
    return make_weights(key)[1].astype(jnp.bfloat16)


def draw_states(key, part):
    base = jax.random.fold_in(key, 23)
    noise = jax.random.normal(jax.random.fold_in(base, 1), (STEPS, TOKENS, D), jnp.float32)
    return jnp.clip(noise, -6.0, 6.0).astype(jnp.bfloat16)


def scatter_about(own_key, extent, deviation, most, kind=jnp.bfloat16):
    drawn = jax.random.normal(own_key, extent, jnp.float32) * deviation
    return jnp.minimum(jnp.maximum(drawn, -most), most).astype(kind)


def setup_inputs(seed: int = 0) -> dict:
    splits = jax.random.split(jax.random.key(seed), 5)
    states = draw_states(jax.random.fold_in(splits[4], 71), 0)
    w_query = draw_w_query(jax.random.fold_in(splits[4], 71), 0)
    w_key = draw_w_key(jax.random.fold_in(splits[4], 71), 0)
    w_value = scatter_about(splits[3], (D, KW), D ** -0.5, 0.125)
    return dict(states=states, w_query=w_query, w_key=w_key, w_value=w_value)


def project(rows, weight):
    return jnp.dot(rows, weight, preferred_element_type=jnp.float32).astype(jnp.bfloat16)

def band_block(q_block, k_block, v_block, base):
    group = HQ // HK
    q_heads = q_block.reshape(TOK_DEV, HK, group, HD).astype(jnp.float32)
    k_heads = k_block.reshape(TOK_DEV + WINDOW, HK, HD).astype(jnp.float32)
    v_heads = v_block.reshape(TOK_DEV + WINDOW, HK, HD).astype(jnp.float32)
    scores = jnp.einsum('qkgd,lkd->kgql', q_heads, k_heads) / jnp.sqrt(jnp.float32(HD))
    qpos = jnp.arange(TOK_DEV, dtype=jnp.int32)[:, None]
    kidx = jnp.arange(TOK_DEV + WINDOW, dtype=jnp.int32)[None, :]
    allowed = (kidx >= qpos) & (kidx <= qpos + WINDOW) & (base - WINDOW + kidx >= 0)
    scores = jnp.where(allowed, scores, -jnp.inf)
    top = lax.optimization_barrier(jnp.max(scores, axis=-1, keepdims=True))
    expo = jnp.exp(scores - top)
    weight = (expo / lax.optimization_barrier(jnp.sum(expo, axis=-1, keepdims=True))).astype(jnp.bfloat16)
    out = jnp.einsum('kgql,lkd->qkgd', weight.astype(jnp.float32), v_heads)
    return out.astype(jnp.bfloat16).reshape(TOK_DEV, QW)

def band_step(q_all, k_all, v_all):
    pad = jnp.zeros((WINDOW, KW), jnp.bfloat16)
    k_pad = jnp.concatenate([pad, k_all], axis=0)
    v_pad = jnp.concatenate([pad, v_all], axis=0)

    def one_block(index):
        base = index * TOK_DEV
        q_block = lax.dynamic_slice_in_dim(q_all, base, TOK_DEV, 0)
        k_block = lax.dynamic_slice_in_dim(k_pad, base, TOK_DEV + WINDOW, 0)
        v_block = lax.dynamic_slice_in_dim(v_pad, base, TOK_DEV + WINDOW, 0)
        return band_block(q_block, k_block, v_block, base)
    blocks = lax.map(one_block, jnp.arange(TOKENS // TOK_DEV, dtype=jnp.int32))
    return blocks.reshape(TOKENS, QW)

def reference(states, w_query, w_key, w_value):

    def per_step(rows):
        return (project(rows, w_query), project(rows, w_key), project(rows, w_value))
    query, key, value = lax.map(per_step, states)
    window_out = lax.map(lambda item: band_step(item[0], item[1], item[2]), (query, key, value))
    group = HQ // HK
    final_q = query[STEPS - 1].reshape(TOKENS, HK, group, HD).astype(jnp.float32)
    k_steps = key.reshape(STEPS, TOKENS, HK, HD).astype(jnp.float32)
    v_steps = value.reshape(STEPS, TOKENS, HK, HD).astype(jnp.float32)
    scores = jnp.einsum('tkgd,stkd->tkgs', final_q, k_steps) / jnp.sqrt(jnp.float32(HD))
    top = lax.optimization_barrier(jnp.max(scores, axis=-1, keepdims=True))
    expo = jnp.exp(scores - top)
    weight = expo / lax.optimization_barrier(jnp.sum(expo, axis=-1, keepdims=True))
    depth_out = jnp.einsum('tkgs,stkd->tkgd', weight, v_steps).astype(jnp.bfloat16).reshape(TOKENS, QW)
    return (window_out, depth_out)
```

```python
import math

import jax
import jax.numpy as jnp
from jax import lax
from jax.experimental import pallas as pl
from jax.experimental.pallas import tpu as pltpu
from jax.sharding import PartitionSpec as P

HQ = 8
HK = 2
HD = 128
GROUP = HQ // HK
WINDOW = 256
D = 2048
QW = HQ * HD
KW = HK * HD
TOK = 1024
STEPS = 16
OWN = TOK // STEPS
CHUNK = 256
BQ = 128
KEYS = BQ + WINDOW
RELAY = 7
LAST = STEPS - 1
SCALE = math.log2(math.e) / math.sqrt(HD)
MESH = pl.DeviceIdType.MESH
F32 = jnp.float32
BF16 = jnp.bfloat16


def softmax_values(scores, values):
    top = jnp.max(scores, axis=-1, keepdims=True)
    weight = jnp.exp2((scores - top) * SCALE).astype(BF16)
    ext = jnp.concatenate([values, jnp.ones_like(values)], axis=1)
    out = jnp.dot(weight, ext, preferred_element_type=F32)
    return out[:, :HD] / out[:, HD:]


def score(rows, keys):
    return lax.dot_general(rows, keys, (((1,), (1,)), ((), ())), preferred_element_type=F32)


def kernel(
    x_hbm, wq_hbm, wk_hbm, wv_hbm, win_hbm, dep_hbm,
    x, wq, wkv, q, kv, kvr, qr, relay, out, dout, bias,
    ld, st, ss, rs, qs_sem, qr_sem, rel_sem, halo_s, halo_r,
):
    me = lax.axis_index("depth")
    shard = lax.axis_index("tok")
    shards = lax.axis_size("tok")
    x_lo = me // 8
    z_hi = (me // 4) % 2
    has_next = shard < shards - 1
    has_prev = shard > 0

    def chunk_of(i):
        return 2 * ((x_lo + 1 - i % 2) % 2) + (z_hi + 1 - i // 2) % 2

    def chunk_rows(i):
        return pl.ds(pl.multiple_of(chunk_of(i) * CHUNK, CHUNK), CHUNK)

    def load_x(i):
        rows = chunk_rows(i)
        return pltpu.make_async_copy(x_hbm.at[rows], x.at[rows], ld.at[i])

    load_k = pltpu.make_async_copy(wk_hbm, wkv.at[:, :KW], ld.at[4])
    load_v = pltpu.make_async_copy(wv_hbm, wkv.at[:, KW:], ld.at[5])
    load_q = pltpu.make_async_copy(wq_hbm, wq, ld.at[6])
    load_k.start()
    load_v.start()
    for i in range(4):
        load_x(i).start()
    load_q.start()

    barrier = pltpu.get_barrier_semaphore()
    for step in range(1, STEPS):
        pl.semaphore_signal(
            barrier, inc=1, device_id={"depth": lax.rem(me + step, STEPS)}, device_id_type=MESH
        )

    @pl.when(has_next)
    def _():
        pl.semaphore_signal(barrier, inc=1, device_id={"tok": shard + 1}, device_id_type=MESH)

    @pl.when(has_prev)
    def _():
        pl.semaphore_signal(barrier, inc=1, device_id={"tok": shard - 1}, device_id_type=MESH)

    row = lax.broadcasted_iota(jnp.int32, (BQ, KEYS), 0)
    col = lax.broadcasted_iota(jnp.int32, (BQ, KEYS), 1)
    band = (col >= row) & (col <= row + WINDOW)
    bias[0] = jnp.where(band, 0.0, -jnp.inf).astype(F32)
    for b in range(2):
        known = col + (b * BQ - WINDOW) + shard * TOK >= 0
        bias[1 + b] = jnp.where(band & known, 0.0, -jnp.inf).astype(F32)

    @pl.when(shard == 0)
    def _():
        kv[:WINDOW] = jnp.zeros((WINDOW, 2 * KW), BF16)

    load_k.wait()
    load_v.wait()

    def project_kv(i, carry):
        load_x(i).wait()
        rows = chunk_rows(i)
        kv[pl.ds(pl.multiple_of(WINDOW + chunk_of(i) * CHUNK, CHUNK), CHUNK)] = jnp.dot(
            x[rows], wkv[...], preferred_element_type=F32
        ).astype(BF16)
        return carry

    lax.fori_loop(0, 4, project_kv, 0)

    pl.semaphore_wait(
        barrier, STEPS - 1 + has_next.astype(jnp.int32) + has_prev.astype(jnp.int32)
    )

    def kv_copy(dest, source):
        rows = pl.ds(pl.multiple_of(WINDOW + dest * OWN, OWN), OWN)
        return pltpu.make_async_remote_copy(
            kv.at[rows], kvr.at[source], ss.at[dest], rs.at[source],
            device_id={"depth": dest}, device_id_type=MESH,
        )

    def send_kv(i):
        for j in range(4):
            dest = chunk_of(i) * 4 + j

            @pl.when(dest != me)
            def _():
                kv_copy(dest, me).start()

    halo = pltpu.make_async_remote_copy(
        kv.at[pl.ds(TOK, WINDOW)], kv.at[pl.ds(0, WINDOW)], halo_s, halo_r,
        device_id={"tok": lax.rem(shard + 1, shards)}, device_id_type=MESH,
    )

    def project_q(i):
        rows = pl.ds(pl.multiple_of(i * CHUNK, CHUNK), CHUNK)
        for n in range(2):
            cols = slice(n * 512, (n + 1) * 512)
            q[rows, cols] = jnp.dot(x[rows], wq[:, cols], preferred_element_type=F32).astype(BF16)

    def q_direct(dest):
        return pltpu.make_async_remote_copy(
            q.at[pl.ds(pl.multiple_of(dest * OWN, OWN), OWN)], qr, qs_sem.at[dest], qr_sem,
            device_id={"depth": dest}, device_id_type=MESH,
        )

    def q_to_relay(dest):
        return pltpu.make_async_remote_copy(
            q.at[pl.ds(pl.multiple_of(dest * OWN, OWN), OWN)], relay.at[dest],
            qs_sem.at[dest], rel_sem.at[dest],
            device_id={"depth": RELAY}, device_id_type=MESH,
        )

    def q_from_relay(dest):
        return pltpu.make_async_remote_copy(
            relay.at[dest], qr, qs_sem.at[dest], qr_sem,
            device_id={"depth": dest}, device_id_type=MESH,
        )

    for i in range(3):
        send_kv(i)
    load_q.wait()
    project_q(0)
    send_kv(3)

    @pl.when(has_next)
    def _():
        halo.start()

    project_q(1)

    @pl.when(me == LAST)
    def _():
        for j in range(4):
            q_to_relay(j).start()

    project_q(2)

    @pl.when(me == LAST)
    def _():
        for j in range(4, RELAY):
            q_to_relay(j).start()
        q_direct(RELAY).start()

    project_q(3)

    @pl.when(me == LAST)
    def _():
        for j in range(8, 12):
            q_direct(j).start()

    kvr[me] = kv[pl.ds(pl.multiple_of(WINDOW + me * OWN, OWN), OWN)]

    @pl.when(me == LAST)
    def _():
        qr[...] = q[pl.ds(LAST * OWN, OWN)]

    def attend(b, edge):
        base = pl.multiple_of(b * BQ, BQ)
        for c in range(HK):
            heads = [
                q[pl.ds(base, BQ), h * HD : (h + 1) * HD] for h in range(c * GROUP, (c + 1) * GROUP)
            ]
            rows = jnp.concatenate(heads, axis=0)
            keys = kv[pl.ds(base, KEYS), c * HD : (c + 1) * HD]
            values = kv[pl.ds(base, KEYS), KW + c * HD : KW + (c + 1) * HD]
            scores = score(rows, keys).reshape(GROUP, BQ, KEYS)
            if edge:
                scores = scores + bias[1 + b][None]
            else:
                scores = jnp.concatenate(
                    [
                        scores[:, :, :BQ] + bias[0, :, :BQ][None],
                        scores[:, :, BQ:WINDOW],
                        scores[:, :, WINDOW:] + bias[0, :, WINDOW:][None],
                    ],
                    axis=-1,
                )
            res = softmax_values(scores.reshape(GROUP * BQ, KEYS), values).astype(BF16)
            for g in range(GROUP):
                h = c * GROUP + g
                out[pl.ds(base, BQ), h * HD : (h + 1) * HD] = res[g * BQ : (g + 1) * BQ]

    def store(b):
        rows = pl.ds(pl.multiple_of(b * BQ, BQ), BQ)
        return pltpu.make_async_copy(out.at[rows], win_hbm.at[rows], st.at[b])

    def forward(i):
        @pl.when(me == RELAY)
        def _():
            q_to_relay(i).wait_recv()
            q_from_relay(i).start()

    def block(i, carry):
        attend(i + 2, False)

        @pl.when(i > 0)
        def _():
            store(i + 1).start()

        @pl.when((me == LAST) & (i == 0))
        def _():
            for j in range(12, LAST):
                q_direct(j).start()

        forward(i)
        return carry

    lax.fori_loop(0, 6, block, 0)
    forward(6)

    @pl.when(has_prev)
    def _():
        halo.wait_recv()

    attend(0, True)
    store(7).start()
    attend(1, True)
    store(0).start()

    for source in range(STEPS):

        @pl.when(me != source)
        def _():
            kv_copy(source, source).wait_recv()

    @pl.when(me != LAST)
    def _():
        q_direct(LAST).wait_recv()

    store(1).start()
    token = lax.broadcasted_iota(jnp.int32, (OWN, STEPS * OWN), 0)
    other = lax.broadcasted_iota(jnp.int32, (OWN, STEPS * OWN), 1) % OWN
    for c in range(HK):
        rows = jnp.concatenate(
            [qr[:, h * HD : (h + 1) * HD] for h in range(c * GROUP, (c + 1) * GROUP)], axis=0
        )
        keys = kvr[:, :, c * HD : (c + 1) * HD].reshape(STEPS * OWN, HD)
        values = kvr[:, :, KW + c * HD : KW + (c + 1) * HD].reshape(STEPS * OWN, HD)
        scores = score(rows, keys).reshape(GROUP, OWN, STEPS * OWN)
        scores = jnp.where((token == other)[None], scores, -jnp.inf)
        res = softmax_values(scores.reshape(GROUP * OWN, STEPS * OWN), values).astype(BF16)
        for g in range(GROUP):
            h = c * GROUP + g
            dout[:, h * HD : (h + 1) * HD] = res[g * OWN : (g + 1) * OWN]

    last = pltpu.make_async_copy(dout, dep_hbm, ld.at[0])
    last.start()
    for dest in range(STEPS):

        @pl.when(me != dest)
        def _():
            kv_copy(dest, dest).wait_send()

    @pl.when(has_next)
    def _():
        halo.wait_send()

    @pl.when(me == LAST)
    def _():
        for dest in range(LAST):
            q_direct(dest).wait_send()

    @pl.when(me == RELAY)
    def _():
        for dest in range(RELAY):
            q_from_relay(dest).wait_send()

    for b in range(TOK // BQ):
        store(b).wait()
    last.wait()


def body(states, w_query, w_key, w_value):
    any_spec = pl.BlockSpec(memory_space=pl.ANY)
    dma = pltpu.SemaphoreType.DMA
    window_out, depth_out = pl.pallas_call(
        kernel,
        out_shape=(
            jax.ShapeDtypeStruct((TOK, QW), BF16),
            jax.ShapeDtypeStruct((OWN, QW), BF16),
        ),
        in_specs=[any_spec] * 4,
        out_specs=(any_spec, any_spec),
        scratch_shapes=[
            pltpu.VMEM((TOK, D), BF16),
            pltpu.VMEM((D, QW), BF16),
            pltpu.VMEM((D, 2 * KW), BF16),
            pltpu.VMEM((TOK, QW), BF16),
            pltpu.VMEM((WINDOW + TOK, 2 * KW), BF16),
            pltpu.VMEM((STEPS, OWN, 2 * KW), BF16),
            pltpu.VMEM((OWN, QW), BF16),
            pltpu.VMEM((RELAY, OWN, QW), BF16),
            pltpu.VMEM((TOK, QW), BF16),
            pltpu.VMEM((OWN, QW), BF16),
            pltpu.VMEM((3, BQ, KEYS), F32),
            dma((7,)),
            dma((TOK // BQ,)),
            dma((STEPS,)),
            dma((STEPS,)),
            dma((STEPS,)),
            dma(()),
            dma((RELAY,)),
            dma(()),
            dma(()),
        ],
        compiler_params=pltpu.CompilerParams(
            collective_id=0, has_side_effects=True, vmem_limit_bytes=60 * 1024 * 1024
        ),
        name="looped_attention",
    )(states[0], w_query, w_key, w_value)
    return (window_out[None], depth_out)


def solution(mesh):
    in_specs = (P("depth", "tok", None), P(), P(), P())
    out_specs = (P("depth", "tok", None), P(("tok", "depth"), None))
    return jax.shard_map(body, mesh=mesh, in_specs=in_specs, out_specs=out_specs, check_vma=False)
```

```python
import math

import jax
import jax.numpy as jnp
from jax import lax
from jax.experimental import pallas as pl
from jax.experimental.pallas import tpu as pltpu
from jax.sharding import PartitionSpec as P

HQ = 8
HK = 2
HD = 128
GROUP = HQ // HK
WINDOW = 256
D = 2048
QW = HQ * HD
KW = HK * HD
TOK = 1024
STEPS = 16
OWN = TOK // STEPS
CHUNK = 256
BQ = 128
KEYS = BQ + WINDOW
RELAY = 7
RELAYED = (3, 2, 4, 1, 5, 6)
DIRECT0 = (0, 7)
LAST = STEPS - 1
SCALE = math.log2(math.e) / math.sqrt(HD)
MESH = pl.DeviceIdType.MESH
F32 = jnp.float32
BF16 = jnp.bfloat16


def softmax_values(scores, values):
    top = jnp.max(scores, axis=-1, keepdims=True)
    weight = jnp.exp2((scores - top) * SCALE).astype(BF16)
    ext = jnp.concatenate([values, jnp.ones_like(values)], axis=1)
    out = jnp.dot(weight, ext, preferred_element_type=F32)
    return out[:, :HD] / out[:, HD:]


def score(rows, keys):
    return lax.dot_general(rows, keys, (((1,), (1,)), ((), ())), preferred_element_type=F32)


def kernel(
    x_hbm, wq_hbm, wk_hbm, wv_hbm, out, kvr, qr,
    x, wq, wkv, q, kv, relay, legs, bias,
    ld, ss, rs, legs_s, legs_r, qs_sem, qr_sem, rel_sem, halo_s, halo_r,
):
    me = lax.axis_index("depth")
    shard = lax.axis_index("tok")
    shards = lax.axis_size("tok")
    x_lo = me // 8
    z_hi = (me // 4) % 2
    has_next = shard < shards - 1
    has_prev = shard > 0

    def chunk_of(i):
        return 2 * ((x_lo + 1 - i % 2) % 2) + (z_hi + 1 - i // 2) % 2

    def chunk_rows(i):
        return pl.ds(pl.multiple_of(chunk_of(i) * CHUNK, CHUNK), CHUNK)

    def load_x(i):
        rows = chunk_rows(i)
        return pltpu.make_async_copy(x_hbm.at[rows], x.at[rows], ld.at[i])

    load_k = pltpu.make_async_copy(wk_hbm, wkv.at[:, :KW], ld.at[4])
    load_v = pltpu.make_async_copy(wv_hbm, wkv.at[:, KW:], ld.at[5])
    load_q = pltpu.make_async_copy(wq_hbm, wq, ld.at[6])
    is_last = me == LAST

    @pl.when(is_last)
    def _():
        load_k.start()
        load_v.start()
        for i in (3, 0, 2, 1):
            load_x(i).start()
        load_q.start()

    @pl.when(me != LAST)
    def _():
        load_k.start()
        load_v.start()
        for i in range(4):
            load_x(i).start()

    barrier = pltpu.get_barrier_semaphore()
    for step in range(1, STEPS):
        pl.semaphore_signal(
            barrier, inc=1, device_id={"depth": lax.rem(me + step, STEPS)}, device_id_type=MESH
        )

    @pl.when(has_next)
    def _():
        pl.semaphore_signal(barrier, inc=1, device_id={"tok": shard + 1}, device_id_type=MESH)

    @pl.when(has_prev)
    def _():
        pl.semaphore_signal(barrier, inc=1, device_id={"tok": shard - 1}, device_id_type=MESH)

    @pl.when(shard == 0)
    def _():
        kv[:WINDOW] = jnp.zeros((WINDOW, 2 * KW), BF16)

    def project_kv(i, carry):
        kv[pl.ds(pl.multiple_of(WINDOW + chunk_of(i) * CHUNK, CHUNK), CHUNK)] = jnp.dot(
            x[chunk_rows(i)], wkv[...], preferred_element_type=F32
        ).astype(BF16)
        return carry

    def project_q(i):
        rows = pl.ds(pl.multiple_of(i * CHUNK, CHUNK), CHUNK)
        for n in range(2):
            cols = slice(n * 512, (n + 1) * 512)
            q[rows, cols] = jnp.dot(x[rows], wq[:, cols], preferred_element_type=F32).astype(BF16)

    def project_q_loop(i, carry):
        project_q(i)
        return carry

    def own_rows(dest):
        return pl.ds(pl.multiple_of(WINDOW + dest * OWN, OWN), OWN)

    def kv_copy(dest, source):
        return pltpu.make_async_remote_copy(
            kv.at[own_rows(dest)], kvr.at[source], ss.at[dest], rs.at[source],
            device_id={"depth": dest}, device_id_type=MESH,
        )

    z = me % 8
    detour = (z == 1) | (z == 4)
    detour_to = jnp.where(z == 1, 5, 0)
    via = x_lo * 8 + jnp.where(z == 1, 3, 2)
    between = (z == 3) | (z == 2)
    between_src = x_lo * 8 + jnp.where(z == 3, 1, 4)
    between_dst = jnp.where(z == 3, 5, 0)

    def first_leg(slot):
        return pltpu.make_async_remote_copy(
            kv.at[own_rows(slot * 8 + detour_to)], legs.at[slot],
            ss.at[slot * 8 + detour_to], legs_r.at[slot],
            device_id={"depth": via}, device_id_type=MESH,
        )

    def second_leg(slot):
        return pltpu.make_async_remote_copy(
            legs.at[slot], kvr.at[between_src], legs_s.at[slot], rs.at[between_src],
            device_id={"depth": slot * 8 + between_dst}, device_id_type=MESH,
        )

    def send_kv(i):
        for j in range(4):
            dest = chunk_of(i) * 4 + j

            in_legs = detour & (dest % 8 == detour_to)

            @pl.when((dest != me) & ~in_legs)
            def _():
                kv_copy(dest, me).start()

            @pl.when(in_legs)
            def _():
                first_leg(dest // 8).start()

    halo = pltpu.make_async_remote_copy(
        kv.at[pl.ds(TOK, WINDOW)], kv.at[pl.ds(0, WINDOW)], halo_s, halo_r,
        device_id={"tok": lax.rem(shard + 1, shards)}, device_id_type=MESH,
    )

    def q_rows(dest):
        return pl.ds(pl.multiple_of(dest * OWN, OWN), OWN)

    def q_direct(dest):
        return pltpu.make_async_remote_copy(
            q.at[q_rows(dest)], qr, qs_sem.at[dest], qr_sem,
            device_id={"depth": dest}, device_id_type=MESH,
        )

    def q_to_relay(dest):
        return pltpu.make_async_remote_copy(
            q.at[q_rows(dest)], relay.at[dest], qs_sem.at[dest], rel_sem.at[dest],
            device_id={"depth": RELAY}, device_id_type=MESH,
        )

    def q_from_relay(dest):
        return pltpu.make_async_remote_copy(
            relay.at[dest], qr, qs_sem.at[dest], qr_sem,
            device_id={"depth": dest}, device_id_type=MESH,
        )

    @pl.when(me != LAST)
    def _():
        load_k.wait()
        load_v.wait()

        def wait_and_project(i, carry):
            load_x(i).wait()
            return project_kv(i, carry)

        lax.fori_loop(0, 4, wait_and_project, 0)
        load_q.start()

    @pl.when(is_last)
    def _():
        load_k.wait()
        load_v.wait()
        load_x(3).wait()
        project_kv(3, 0)
        load_q.wait()
        for i in range(3):
            load_x(i).wait()
        lax.fori_loop(0, 2, project_q_loop, 0)

    pl.semaphore_wait(
        barrier, STEPS - 1 + has_next.astype(jnp.int32) + has_prev.astype(jnp.int32)
    )

    @pl.when(has_next)
    def _():
        halo.start()

    @pl.when(me != LAST)
    def _():
        for i in range(3):
            send_kv(i)
        load_q.wait()
        project_q(0)
        send_kv(3)
        lax.fori_loop(1, 4, project_q_loop, 0)

    @pl.when(is_last)
    def _():
        for dest in RELAYED:
            q_to_relay(dest).start()
        for dest in DIRECT0:
            q_direct(dest).start()
        lax.fori_loop(0, 3, project_kv, 0)
        lax.fori_loop(2, 3, project_q_loop, 0)
        for dest in (11, 10, 9, 8):
            q_direct(dest).start()
        for i in range(4):
            send_kv(i)
        lax.fori_loop(3, 4, project_q_loop, 0)
        qr[...] = q[pl.ds(LAST * OWN, OWN)]

    kvr[me] = kv[own_rows(me)]

    row = lax.broadcasted_iota(jnp.int32, (BQ, KEYS), 0)
    col = lax.broadcasted_iota(jnp.int32, (BQ, KEYS), 1)
    band = (col >= row) & (col <= row + WINDOW)
    bias[0] = jnp.where(band, 0.0, -jnp.inf).astype(F32)
    for b in range(2):
        known = col + (b * BQ - WINDOW) + shard * TOK >= 0
        bias[1 + b] = jnp.where(band & known, 0.0, -jnp.inf).astype(F32)

    def attend(b, edge):
        base = pl.multiple_of(b * BQ, BQ)
        for c in range(HK):
            heads = [
                q[pl.ds(base, BQ), h * HD : (h + 1) * HD] for h in range(c * GROUP, (c + 1) * GROUP)
            ]
            rows = jnp.concatenate(heads, axis=0)
            keys = kv[pl.ds(base, KEYS), c * HD : (c + 1) * HD]
            values = kv[pl.ds(base, KEYS), KW + c * HD : KW + (c + 1) * HD]
            scores = score(rows, keys).reshape(GROUP, BQ, KEYS)
            if edge:
                scores = scores + bias[1 + b][None]
            else:
                scores = jnp.concatenate(
                    [
                        scores[:, :, :BQ] + bias[0, :, :BQ][None],
                        scores[:, :, BQ:WINDOW],
                        scores[:, :, WINDOW:] + bias[0, :, WINDOW:][None],
                    ],
                    axis=-1,
                )
            res = softmax_values(scores.reshape(GROUP * BQ, KEYS), values).astype(BF16)
            for g in range(GROUP):
                h = c * GROUP + g
                out[pl.ds(base, BQ), h * HD : (h + 1) * HD] = res[g * BQ : (g + 1) * BQ]

    def forward(i):
        @pl.when(me == RELAY)
        def _():
            q_to_relay(RELAYED[i]).wait_recv()
            q_from_relay(RELAYED[i]).start()

    for i in range(6):
        attend(i + 2, False)
        if i == 0:

            @pl.when(is_last)
            def _():
                for dest in (12, 13, 14):
                    q_direct(dest).start()

        if i == 1:

            @pl.when(between)
            def _():
                for slot in range(2):
                    first_leg(slot).wait_recv()
                    second_leg(slot).start()

        if i < len(RELAYED):
            forward(i)
    for i in range(6, len(RELAYED)):
        forward(i)

    @pl.when(has_prev)
    def _():
        halo.wait_recv()

    attend(0, True)
    attend(1, True)

    for source in range(STEPS):

        @pl.when(me != source)
        def _():
            kv_copy(source, source).wait_recv()

    @pl.when(me != LAST)
    def _():
        q_direct(LAST).wait_recv()

    for dest in range(STEPS):

        @pl.when(me != dest)
        def _():
            kv_copy(dest, dest).wait_send()

    @pl.when(has_next)
    def _():
        halo.wait_send()

    @pl.when(me == LAST)
    def _():
        for dest in range(LAST):
            q_direct(dest).wait_send()

    @pl.when(me == RELAY)
    def _():
        for dest in RELAYED:
            q_from_relay(dest).wait_send()

    @pl.when(between)
    def _():
        for slot in range(2):
            second_leg(slot).wait_send()


def finish(out, kvr, qr, win_hbm, dep_hbm, dout, sem):
    window = pltpu.make_async_copy(out, win_hbm, sem.at[0])
    window.start()
    token = lax.broadcasted_iota(jnp.int32, (OWN, STEPS * OWN), 0)
    other = lax.broadcasted_iota(jnp.int32, (OWN, STEPS * OWN), 1) % OWN
    for c in range(HK):
        rows = jnp.concatenate(
            [qr[:, h * HD : (h + 1) * HD] for h in range(c * GROUP, (c + 1) * GROUP)], axis=0
        )
        keys = kvr[:, :, c * HD : (c + 1) * HD].reshape(STEPS * OWN, HD)
        values = kvr[:, :, KW + c * HD : KW + (c + 1) * HD].reshape(STEPS * OWN, HD)
        scores = score(rows, keys).reshape(GROUP, OWN, STEPS * OWN)
        scores = jnp.where((token == other)[None], scores, -jnp.inf)
        res = softmax_values(scores.reshape(GROUP * OWN, STEPS * OWN), values).astype(BF16)
        for g in range(GROUP):
            h = c * GROUP + g
            dout[:, h * HD : (h + 1) * HD] = res[g * OWN : (g + 1) * OWN]

    last = pltpu.make_async_copy(dout, dep_hbm, sem.at[1])
    last.start()
    window.wait()
    last.wait()


def body(states, w_query, w_key, w_value):
    any_spec = pl.BlockSpec(memory_space=pltpu.HBM)
    dma = pltpu.SemaphoreType.DMA
    args = [
        pltpu.with_memory_space_constraint(a, pltpu.HBM)
        for a in (states[0], w_query, w_key, w_value)
    ]
    vmem = pl.BlockSpec(memory_space=pltpu.VMEM)
    local = pl.pallas_call(
        kernel,
        out_shape=(
            jax.ShapeDtypeStruct((TOK, QW), BF16),
            jax.ShapeDtypeStruct((STEPS, OWN, 2 * KW), BF16),
            jax.ShapeDtypeStruct((OWN, QW), BF16),
        ),
        in_specs=[any_spec] * 4,
        out_specs=(vmem, vmem, vmem),
        scratch_shapes=[
            pltpu.VMEM((TOK, D), BF16),
            pltpu.VMEM((D, QW), BF16),
            pltpu.VMEM((D, 2 * KW), BF16),
            pltpu.VMEM((TOK, QW), BF16),
            pltpu.VMEM((WINDOW + TOK, 2 * KW), BF16),
            pltpu.VMEM((RELAY, OWN, QW), BF16),
            pltpu.VMEM((2, OWN, 2 * KW), BF16),
            pltpu.VMEM((3, BQ, KEYS), F32),
            dma((7,)),
            dma((STEPS,)),
            dma((STEPS,)),
            dma((2,)),
            dma((2,)),
            dma((STEPS,)),
            dma(()),
            dma((RELAY,)),
            dma(()),
            dma(()),
        ],
        compiler_params=pltpu.CompilerParams(
            collective_id=0, has_side_effects=True, vmem_limit_bytes=40 * 1024 * 1024
        ),
        name="looped_attention",
    )(*args)
    window_out, depth_out = pl.pallas_call(
        finish,
        out_shape=(
            jax.ShapeDtypeStruct((TOK, QW), BF16),
            jax.ShapeDtypeStruct((OWN, QW), BF16),
        ),
        in_specs=[vmem] * 3,
        out_specs=(any_spec, any_spec),
        scratch_shapes=[pltpu.VMEM((OWN, QW), BF16), dma((2,))],
        compiler_params=pltpu.CompilerParams(vmem_limit_bytes=16 * 1024 * 1024),
        name="final_attention",
    )(*local)
    return (window_out[None], depth_out)


def solution(mesh):
    in_specs = (P("depth", "tok", None), P(), P(), P())
    out_specs = (P("depth", "tok", None), P(("tok", "depth"), None))
    return jax.shard_map(body, mesh=mesh, in_specs=in_specs, out_specs=out_specs, check_vma=False)
```

```python
import math

import jax
import jax.numpy as jnp
from jax import lax
from jax.experimental import pallas as pl
from jax.experimental.pallas import tpu as pltpu
from jax.sharding import PartitionSpec as P

HQ = 8
HK = 2
HD = 128
GROUP = HQ // HK
WINDOW = 256
D = 2048
QW = HQ * HD
KW = HK * HD
TOK = 1024
STEPS = 16
OWN = TOK // STEPS
CHUNK = 256
BQ = 128
KEYS = BQ + WINDOW
RELAY = 7
RELAYED = (0, 2, 1, 3, 4, 5, 6)
SIDE = (0, 1, 5, 6)
LAST = STEPS - 1
SCALE = math.log2(math.e) / math.sqrt(HD)
MESH = pl.DeviceIdType.MESH
F32 = jnp.float32
BF16 = jnp.bfloat16


def softmax_values(scores, values):
    top = jnp.max(scores, axis=-1, keepdims=True)
    weight = jnp.exp2((scores - top) * SCALE).astype(BF16)
    ext = jnp.concatenate([values, jnp.ones_like(values)], axis=1)
    out = jnp.dot(weight, ext, preferred_element_type=F32)
    return out[:, :HD] / out[:, HD:]


def score(rows, keys):
    return lax.dot_general(rows, keys, (((1,), (1,)), ((), ())), preferred_element_type=F32)


def kernel(
    x_hbm, wq_hbm, wk_hbm, wv_hbm, out, kvr, qr,
    x, wq, wkv, q, kv, relay, legs, bias,
    ld, ss, rs, legs_s, legs_r, qs_sem, qr_sem, rel_sem, halo_s, halo_r,
):
    me = lax.axis_index("depth")
    shard = lax.axis_index("tok")
    shards = lax.axis_size("tok")
    x_lo = me // 8
    z_hi = (me // 4) % 2
    has_next = shard < shards - 1
    has_prev = shard > 0

    def chunk_of(i):
        return 2 * ((x_lo + 1 - i % 2) % 2) + (z_hi + 1 - i // 2) % 2

    def chunk_rows(i):
        return pl.ds(pl.multiple_of(chunk_of(i) * CHUNK, CHUNK), CHUNK)

    def load_x(i):
        rows = chunk_rows(i)
        return pltpu.make_async_copy(x_hbm.at[rows], x.at[rows], ld.at[i])

    load_k = pltpu.make_async_copy(wk_hbm, wkv.at[:, :KW], ld.at[4])
    load_v = pltpu.make_async_copy(wv_hbm, wkv.at[:, KW:], ld.at[5])
    load_q = pltpu.make_async_copy(wq_hbm, wq, ld.at[6])
    is_last = me == LAST

    load_k.start()
    load_v.start()
    for i in range(4):
        load_x(i).start()

    barrier = pltpu.get_barrier_semaphore()
    for step in range(1, STEPS):
        pl.semaphore_signal(
            barrier, inc=1, device_id={"depth": lax.rem(me + step, STEPS)}, device_id_type=MESH
        )

    @pl.when(has_next)
    def _():
        pl.semaphore_signal(barrier, inc=1, device_id={"tok": shard + 1}, device_id_type=MESH)

    @pl.when(has_prev)
    def _():
        pl.semaphore_signal(barrier, inc=1, device_id={"tok": shard - 1}, device_id_type=MESH)

    @pl.when(shard == 0)
    def _():
        kv[:WINDOW] = jnp.zeros((WINDOW, 2 * KW), BF16)

    def project_kv(i):
        kv[pl.ds(pl.multiple_of(WINDOW + chunk_of(i) * CHUNK, CHUNK), CHUNK)] = jnp.dot(
            x[chunk_rows(i)], wkv[...], preferred_element_type=F32
        ).astype(BF16)

    def project_q(i):
        rows = pl.ds(pl.multiple_of(i * CHUNK, CHUNK), CHUNK)
        for n in range(2):
            cols = slice(n * 512, (n + 1) * 512)
            q[rows, cols] = jnp.dot(x[rows], wq[:, cols], preferred_element_type=F32).astype(BF16)

    def own_rows(dest):
        return pl.ds(pl.multiple_of(WINDOW + dest * OWN, OWN), OWN)

    def kv_copy(dest, source):
        return pltpu.make_async_remote_copy(
            kv.at[own_rows(dest)], kvr.at[source], ss.at[dest], rs.at[source],
            device_id={"depth": dest}, device_id_type=MESH,
        )

    z = me % 8
    detour = (z == 1) | (z == 4)
    detour_to = jnp.where(z == 1, 5, 0)
    via = x_lo * 8 + jnp.where(z == 1, 3, 2)
    between = (z == 3) | (z == 2)
    between_src = x_lo * 8 + jnp.where(z == 3, 1, 4)
    between_dst = jnp.where(z == 3, 5, 0)

    def first_leg(slot):
        return pltpu.make_async_remote_copy(
            kv.at[own_rows(slot * 8 + detour_to)], legs.at[slot],
            ss.at[slot * 8 + detour_to], legs_r.at[slot],
            device_id={"depth": via}, device_id_type=MESH,
        )

    def second_leg(slot):
        return pltpu.make_async_remote_copy(
            legs.at[slot], kvr.at[between_src], legs_s.at[slot], rs.at[between_src],
            device_id={"depth": slot * 8 + between_dst}, device_id_type=MESH,
        )

    on_side = z == SIDE[0]
    for s in SIDE[1:]:
        on_side = on_side | (z == s)

    def side_first():
        return pltpu.make_async_remote_copy(
            kv.at[own_rows(RELAY)], legs.at[0], ss.at[RELAY], legs_r.at[0],
            device_id={"depth": z}, device_id_type=MESH,
        )

    def side_second():
        return pltpu.make_async_remote_copy(
            legs.at[0], kvr.at[8 + z], legs_s.at[0], rs.at[8 + z],
            device_id={"depth": RELAY}, device_id_type=MESH,
        )

    def send_kv(i):
        for j in range(4):
            dest = chunk_of(i) * 4 + j

            direct = dest != me
            if j < 2:
                in_legs = detour & (dest % 8 == detour_to)
                direct = direct & ~in_legs

                @pl.when(in_legs)
                def _():
                    first_leg(dest // 8).start()

            if j == 3:
                by_side = on_side & (x_lo == 1) & (dest == RELAY)
                direct = direct & ~by_side

                @pl.when(by_side)
                def _():
                    side_first().start()

            @pl.when(direct)
            def _():
                kv_copy(dest, me).start()

    halo = pltpu.make_async_remote_copy(
        kv.at[pl.ds(TOK, WINDOW)], kv.at[pl.ds(0, WINDOW)], halo_s, halo_r,
        device_id={"tok": lax.rem(shard + 1, shards)}, device_id_type=MESH,
    )

    def q_rows(dest):
        return pl.ds(pl.multiple_of(dest * OWN, OWN), OWN)

    def q_direct(dest):
        return pltpu.make_async_remote_copy(
            q.at[q_rows(dest)], qr, qs_sem.at[dest], qr_sem,
            device_id={"depth": dest}, device_id_type=MESH,
        )

    def q_to_relay(dest):
        return pltpu.make_async_remote_copy(
            q.at[q_rows(dest)], relay.at[dest], qs_sem.at[dest], rel_sem.at[dest],
            device_id={"depth": RELAY}, device_id_type=MESH,
        )

    def q_from_relay(dest):
        return pltpu.make_async_remote_copy(
            relay.at[dest], qr, qs_sem.at[dest], qr_sem,
            device_id={"depth": dest}, device_id_type=MESH,
        )

    load_k.wait()
    load_v.wait()
    load_x(0).wait()
    project_kv(0)
    load_x(1).wait()
    load_q.start()
    project_kv(1)
    pl.semaphore_wait(
        barrier, STEPS - 1 + has_next.astype(jnp.int32) + has_prev.astype(jnp.int32)
    )
    send_kv(0)
    load_x(2).wait()
    project_kv(2)
    send_kv(1)
    load_x(3).wait()
    project_kv(3)
    send_kv(2)

    @pl.when(has_next)
    def _():
        halo.start()

    load_q.wait()
    project_q(0)
    send_kv(3)
    project_q(1)

    @pl.when(is_last)
    def _():
        for dest in (0, 2, 1, 3):
            q_to_relay(dest).start()

    project_q(2)

    @pl.when(is_last)
    def _():
        for dest in (4, 5, 6):
            q_to_relay(dest).start()
        q_direct(RELAY).start()

    project_q(3)

    @pl.when(is_last)
    def _():
        for dest in (10, 9, 8, 11):
            q_direct(dest).start()

    @pl.when(between)
    def _():
        for slot in range(2):
            first_leg(slot).wait_recv()
            second_leg(slot).start()

    @pl.when(on_side & (x_lo == 0))
    def _():
        side_first().wait_recv()
        side_second().start()

    kvr[me] = kv[own_rows(me)]

    @pl.when(is_last)
    def _():
        for dest in (12, 13, 14):
            q_direct(dest).start()
        qr[...] = q[pl.ds(LAST * OWN, OWN)]

    row = lax.broadcasted_iota(jnp.int32, (BQ, KEYS), 0)
    col = lax.broadcasted_iota(jnp.int32, (BQ, KEYS), 1)
    band = (col >= row) & (col <= row + WINDOW)
    bias[0] = jnp.where(band, 0.0, -jnp.inf).astype(F32)
    for b in range(2):
        known = col + (b * BQ - WINDOW) + shard * TOK >= 0
        bias[1 + b] = jnp.where(band & known, 0.0, -jnp.inf).astype(F32)

    def attend(b, edge):
        base = pl.multiple_of(b * BQ, BQ)
        for c in range(HK):
            heads = [
                q[pl.ds(base, BQ), h * HD : (h + 1) * HD] for h in range(c * GROUP, (c + 1) * GROUP)
            ]
            rows = jnp.concatenate(heads, axis=0)
            keys = kv[pl.ds(base, KEYS), c * HD : (c + 1) * HD]
            values = kv[pl.ds(base, KEYS), KW + c * HD : KW + (c + 1) * HD]
            scores = score(rows, keys).reshape(GROUP, BQ, KEYS)
            if edge:
                scores = scores + bias[1 + b][None]
            else:
                scores = jnp.concatenate(
                    [
                        scores[:, :, :BQ] + bias[0, :, :BQ][None],
                        scores[:, :, BQ:WINDOW],
                        scores[:, :, WINDOW:] + bias[0, :, WINDOW:][None],
                    ],
                    axis=-1,
                )
            res = softmax_values(scores.reshape(GROUP * BQ, KEYS), values).astype(BF16)
            for g in range(GROUP):
                h = c * GROUP + g
                out[pl.ds(base, BQ), h * HD : (h + 1) * HD] = res[g * BQ : (g + 1) * BQ]

    def forward(i):
        @pl.when(me == RELAY)
        def _():
            q_to_relay(RELAYED[i]).wait_recv()
            q_from_relay(RELAYED[i]).start()

    forward(0)
    for i in range(6):
        attend(i + 2, False)
        forward(i + 1)

    @pl.when(has_prev)
    def _():
        halo.wait_recv()

    attend(0, True)
    attend(1, True)

    for source in range(STEPS):

        @pl.when(me != source)
        def _():
            kv_copy(source, source).wait_recv()

    @pl.when(me != LAST)
    def _():
        q_direct(LAST).wait_recv()

    for dest in range(STEPS):

        @pl.when(me != dest)
        def _():
            kv_copy(dest, dest).wait_send()

    @pl.when(has_next)
    def _():
        halo.wait_send()

    @pl.when(me == LAST)
    def _():
        for dest in range(LAST):
            q_direct(dest).wait_send()

    @pl.when(me == RELAY)
    def _():
        for dest in RELAYED:
            q_from_relay(dest).wait_send()

    @pl.when(between)
    def _():
        for slot in range(2):
            second_leg(slot).wait_send()

    @pl.when(on_side & (x_lo == 0))
    def _():
        side_second().wait_send()


def finish(out, kvr, qr, win_hbm, dep_hbm, dout, sem):
    window = pltpu.make_async_copy(out, win_hbm, sem.at[0])
    window.start()

    def half(c):
        cols = slice(c * GROUP * HD, (c + 1) * GROUP * HD)
        return pltpu.make_async_copy(dout.at[:, cols], dep_hbm.at[:, cols], sem.at[1 + c])

    token = lax.broadcasted_iota(jnp.int32, (OWN, STEPS * OWN), 0)
    other = lax.broadcasted_iota(jnp.int32, (OWN, STEPS * OWN), 1) % OWN
    for c in range(HK):
        rows = jnp.concatenate(
            [qr[:, h * HD : (h + 1) * HD] for h in range(c * GROUP, (c + 1) * GROUP)], axis=0
        )
        keys = kvr[:, :, c * HD : (c + 1) * HD].reshape(STEPS * OWN, HD)
        values = kvr[:, :, KW + c * HD : KW + (c + 1) * HD].reshape(STEPS * OWN, HD)
        scores = score(rows, keys).reshape(GROUP, OWN, STEPS * OWN)
        scores = jnp.where((token == other)[None], scores, -jnp.inf)
        res = softmax_values(scores.reshape(GROUP * OWN, STEPS * OWN), values).astype(BF16)
        for g in range(GROUP):
            h = c * GROUP + g
            dout[:, h * HD : (h + 1) * HD] = res[g * OWN : (g + 1) * OWN]
        half(c).start()

    window.wait()
    for c in range(HK):
        half(c).wait()


def body(states, w_query, w_key, w_value):
    any_spec = pl.BlockSpec(memory_space=pltpu.HBM)
    dma = pltpu.SemaphoreType.DMA
    args = [
        pltpu.with_memory_space_constraint(a, pltpu.HBM)
        for a in (states[0], w_query, w_key, w_value)
    ]
    vmem = pl.BlockSpec(memory_space=pltpu.VMEM)
    local = pl.pallas_call(
        kernel,
        out_shape=(
            jax.ShapeDtypeStruct((TOK, QW), BF16),
            jax.ShapeDtypeStruct((STEPS, OWN, 2 * KW), BF16),
            jax.ShapeDtypeStruct((OWN, QW), BF16),
        ),
        in_specs=[any_spec] * 4,
        out_specs=(vmem, vmem, vmem),
        scratch_shapes=[
            pltpu.VMEM((TOK, D), BF16),
            pltpu.VMEM((D, QW), BF16),
            pltpu.VMEM((D, 2 * KW), BF16),
            pltpu.VMEM((TOK, QW), BF16),
            pltpu.VMEM((WINDOW + TOK, 2 * KW), BF16),
            pltpu.VMEM((RELAY, OWN, QW), BF16),
            pltpu.VMEM((2, OWN, 2 * KW), BF16),
            pltpu.VMEM((3, BQ, KEYS), F32),
            dma((7,)),
            dma((STEPS,)),
            dma((STEPS,)),
            dma((2,)),
            dma((2,)),
            dma((STEPS,)),
            dma(()),
            dma((RELAY,)),
            dma(()),
            dma(()),
        ],
        compiler_params=pltpu.CompilerParams(
            collective_id=0, has_side_effects=True, vmem_limit_bytes=40 * 1024 * 1024
        ),
        name="looped_attention",
    )(*args)
    window_out, depth_out = pl.pallas_call(
        finish,
        out_shape=(
            jax.ShapeDtypeStruct((TOK, QW), BF16),
            jax.ShapeDtypeStruct((OWN, QW), BF16),
        ),
        in_specs=[vmem] * 3,
        out_specs=(any_spec, any_spec),
        scratch_shapes=[pltpu.VMEM((OWN, QW), BF16), dma((3,))],
        compiler_params=pltpu.CompilerParams(vmem_limit_bytes=16 * 1024 * 1024),
        name="final_attention",
    )(*local)
    return (window_out[None], depth_out)


def solution(mesh):
    in_specs = (P("depth", "tok", None), P(), P(), P())
    out_specs = (P("depth", "tok", None), P(("tok", "depth"), None))
    return jax.shard_map(body, mesh=mesh, in_specs=in_specs, out_specs=out_specs, check_vma=False)
```

```python
import math

import jax
import jax.numpy as jnp
from jax import lax
from jax.experimental import pallas as pl
from jax.experimental.pallas import tpu as pltpu
from jax.sharding import PartitionSpec as P

HQ = 8
HK = 2
HD = 128
GROUP = HQ // HK
WINDOW = 256
D = 2048
QW = HQ * HD
KW = HK * HD
TOK = 1024
STEPS = 16
OWN = TOK // STEPS
CHUNK = 256
BQ = 128
KEYS = BQ + WINDOW
RELAY = 7
RELAYED = (0, 2, 1, 3, 4, 5, 6)
SIDE = (0, 1, 5, 6)
LEGS_AT = 2
LAST = STEPS - 1
SCALE = math.log2(math.e) / math.sqrt(HD)
MESH = pl.DeviceIdType.MESH
F32 = jnp.float32
BF16 = jnp.bfloat16


def softmax_values(scores, values):
    top = jnp.max(scores, axis=-1, keepdims=True)
    weight = jnp.exp2((scores - top) * SCALE).astype(BF16)
    ext = jnp.concatenate([values, jnp.ones_like(values)], axis=1)
    out = jnp.dot(weight, ext, preferred_element_type=F32)
    return out[:, :HD] / out[:, HD:]


def score(rows, keys):
    return lax.dot_general(rows, keys, (((1,), (1,)), ((), ())), preferred_element_type=F32)


def kernel(
    x_hbm, wq_hbm, wk_hbm, wv_hbm, out, kvr, qr,
    x, wq, wkv, q, kv, relay, legs, bias,
    ld, ss, rs, legs_s, legs_r, qs_sem, qr_sem, rel_sem, halo_s, halo_r,
):
    me = lax.axis_index("depth")
    shard = lax.axis_index("tok")
    shards = lax.axis_size("tok")
    x_lo = me // 8
    z_hi = (me // 4) % 2
    has_next = shard < shards - 1
    has_prev = shard > 0

    def chunk_of(i):
        return 2 * ((x_lo + 1 - i % 2) % 2) + (z_hi + 1 - i // 2) % 2

    def chunk_rows(i):
        return pl.ds(pl.multiple_of(chunk_of(i) * CHUNK, CHUNK), CHUNK)

    def load_x(i):
        rows = chunk_rows(i)
        return pltpu.make_async_copy(x_hbm.at[rows], x.at[rows], ld.at[i])

    load_k = pltpu.make_async_copy(wk_hbm, wkv.at[:, :KW], ld.at[4])
    load_v = pltpu.make_async_copy(wv_hbm, wkv.at[:, KW:], ld.at[5])
    load_q = pltpu.make_async_copy(wq_hbm, wq, ld.at[6])
    is_last = me == LAST

    load_k.start()
    load_v.start()
    for i in range(4):
        load_x(i).start()

    barrier = pltpu.get_barrier_semaphore()
    for step in range(1, STEPS):
        pl.semaphore_signal(
            barrier, inc=1, device_id={"depth": lax.rem(me + step, STEPS)}, device_id_type=MESH
        )

    @pl.when(has_next)
    def _():
        pl.semaphore_signal(barrier, inc=1, device_id={"tok": shard + 1}, device_id_type=MESH)

    @pl.when(has_prev)
    def _():
        pl.semaphore_signal(barrier, inc=1, device_id={"tok": shard - 1}, device_id_type=MESH)

    @pl.when(shard == 0)
    def _():
        kv[:WINDOW] = jnp.zeros((WINDOW, 2 * KW), BF16)

    def project_kv(i):
        kv[pl.ds(pl.multiple_of(WINDOW + chunk_of(i) * CHUNK, CHUNK), CHUNK)] = jnp.dot(
            x[chunk_rows(i)], wkv[...], preferred_element_type=F32
        ).astype(BF16)

    def project_q(i):
        rows = pl.ds(pl.multiple_of(i * CHUNK, CHUNK), CHUNK)
        for n in range(2):
            cols = slice(n * 512, (n + 1) * 512)
            q[rows, cols] = jnp.dot(x[rows], wq[:, cols], preferred_element_type=F32).astype(BF16)

    def own_rows(dest):
        return pl.ds(pl.multiple_of(WINDOW + dest * OWN, OWN), OWN)

    def kv_copy(dest, source):
        return pltpu.make_async_remote_copy(
            kv.at[own_rows(dest)], kvr.at[source], ss.at[dest], rs.at[source],
            device_id={"depth": dest}, device_id_type=MESH,
        )

    z = me % 8
    detour = (z == 1) | (z == 4)
    detour_to = jnp.where(z == 1, 5, 0)
    via = x_lo * 8 + jnp.where(z == 1, 3, 2)
    between = (z == 3) | (z == 2)
    between_src = x_lo * 8 + jnp.where(z == 3, 1, 4)
    between_dst = jnp.where(z == 3, 5, 0)

    def first_leg(slot):
        return pltpu.make_async_remote_copy(
            kv.at[own_rows(slot * 8 + detour_to)], legs.at[slot],
            ss.at[slot * 8 + detour_to], legs_r.at[slot],
            device_id={"depth": via}, device_id_type=MESH,
        )

    def second_leg(slot):
        return pltpu.make_async_remote_copy(
            legs.at[slot], kvr.at[between_src], legs_s.at[slot], rs.at[between_src],
            device_id={"depth": slot * 8 + between_dst}, device_id_type=MESH,
        )

    on_side = z == SIDE[0]
    for s in SIDE[1:]:
        on_side = on_side | (z == s)

    def side_first():
        return pltpu.make_async_remote_copy(
            kv.at[own_rows(RELAY)], legs.at[0], ss.at[RELAY], legs_r.at[0],
            device_id={"depth": z}, device_id_type=MESH,
        )

    def side_second():
        return pltpu.make_async_remote_copy(
            legs.at[0], kvr.at[8 + z], legs_s.at[0], rs.at[8 + z],
            device_id={"depth": RELAY}, device_id_type=MESH,
        )

    def send_kv(i):
        for j in range(4):
            dest = chunk_of(i) * 4 + j

            direct = dest != me
            if j < 2:
                in_legs = detour & (dest % 8 == detour_to)
                direct = direct & ~in_legs

                @pl.when(in_legs)
                def _():
                    first_leg(dest // 8).start()

            if j == 3:
                by_side = on_side & (x_lo == 1) & (dest == RELAY)
                direct = direct & ~by_side

                @pl.when(by_side)
                def _():
                    side_first().start()

            @pl.when(direct)
            def _():
                kv_copy(dest, me).start()

    halo = pltpu.make_async_remote_copy(
        kv.at[pl.ds(TOK, WINDOW)], kv.at[pl.ds(0, WINDOW)], halo_s, halo_r,
        device_id={"tok": lax.rem(shard + 1, shards)}, device_id_type=MESH,
    )

    def q_rows(dest):
        return pl.ds(pl.multiple_of(dest * OWN, OWN), OWN)

    def q_direct(dest):
        return pltpu.make_async_remote_copy(
            q.at[q_rows(dest)], qr, qs_sem.at[dest], qr_sem,
            device_id={"depth": dest}, device_id_type=MESH,
        )

    def q_to_relay(dest):
        return pltpu.make_async_remote_copy(
            q.at[q_rows(dest)], relay.at[dest], qs_sem.at[dest], rel_sem.at[dest],
            device_id={"depth": RELAY}, device_id_type=MESH,
        )

    def q_from_relay(dest):
        return pltpu.make_async_remote_copy(
            relay.at[dest], qr, qs_sem.at[dest], qr_sem,
            device_id={"depth": dest}, device_id_type=MESH,
        )

    load_k.wait()
    load_v.wait()
    load_x(0).wait()
    project_kv(0)
    load_x(1).wait()
    load_q.start()
    project_kv(1)
    pl.semaphore_wait(
        barrier, STEPS - 1 + has_next.astype(jnp.int32) + has_prev.astype(jnp.int32)
    )
    send_kv(0)
    load_x(2).wait()
    project_kv(2)
    send_kv(1)
    load_x(3).wait()
    project_kv(3)
    send_kv(2)

    late_halo = is_last & (shard == shards // 2 - 1)

    @pl.when(has_next & ~late_halo)
    def _():
        halo.start()

    load_q.wait()
    project_q(0)
    send_kv(3)
    project_q(1)

    @pl.when(is_last)
    def _():
        for dest in (0, 2, 1, 3):
            q_to_relay(dest).start()

    project_q(2)

    @pl.when(is_last)
    def _():
        for dest in (4, 5, 6):
            q_to_relay(dest).start()

        @pl.when(late_halo)
        def _():
            halo.start()

        q_direct(RELAY).start()

    project_q(3)

    @pl.when(is_last)
    def _():
        for dest in (10, 9, 8, 11):
            q_direct(dest).start()

    kvr[me] = kv[own_rows(me)]

    @pl.when(is_last)
    def _():
        for dest in (12, 13, 14):
            q_direct(dest).start()
        qr[...] = q[pl.ds(LAST * OWN, OWN)]

    row = lax.broadcasted_iota(jnp.int32, (BQ, KEYS), 0)
    col = lax.broadcasted_iota(jnp.int32, (BQ, KEYS), 1)
    band = (col >= row) & (col <= row + WINDOW)
    bias[0] = jnp.where(band, 0.0, -jnp.inf).astype(F32)
    for b in range(2):
        known = col + (b * BQ - WINDOW) + shard * TOK >= 0
        bias[1 + b] = jnp.where(band & known, 0.0, -jnp.inf).astype(F32)

    def attend(b, edge):
        base = pl.multiple_of(b * BQ, BQ)
        for c in range(HK):
            heads = [
                q[pl.ds(base, BQ), h * HD : (h + 1) * HD] for h in range(c * GROUP, (c + 1) * GROUP)
            ]
            rows = jnp.concatenate(heads, axis=0)
            keys = kv[pl.ds(base, KEYS), c * HD : (c + 1) * HD]
            values = kv[pl.ds(base, KEYS), KW + c * HD : KW + (c + 1) * HD]
            scores = score(rows, keys).reshape(GROUP, BQ, KEYS)
            if edge:
                scores = scores + bias[1 + b][None]
            else:
                scores = jnp.concatenate(
                    [
                        scores[:, :, :BQ] + bias[0, :, :BQ][None],
                        scores[:, :, BQ:WINDOW],
                        scores[:, :, WINDOW:] + bias[0, :, WINDOW:][None],
                    ],
                    axis=-1,
                )
            res = softmax_values(scores.reshape(GROUP * BQ, KEYS), values).astype(BF16)
            for g in range(GROUP):
                h = c * GROUP + g
                out[pl.ds(base, BQ), h * HD : (h + 1) * HD] = res[g * BQ : (g + 1) * BQ]

    def forward(i):
        @pl.when(me == RELAY)
        def _():
            q_to_relay(RELAYED[i]).wait_recv()
            q_from_relay(RELAYED[i]).start()

    forward(0)
    for i in range(6):
        attend(i + 2, False)
        if i == LEGS_AT:

            @pl.when(between)
            def _():
                for slot in range(2):
                    first_leg(slot).wait_recv()
                    second_leg(slot).start()

            @pl.when(on_side & (x_lo == 0))
            def _():
                side_first().wait_recv()
                side_second().start()

        forward(i + 1)

    @pl.when(has_prev)
    def _():
        halo.wait_recv()

    attend(0, True)
    attend(1, True)

    for source in range(STEPS):

        @pl.when(me != source)
        def _():
            kv_copy(source, source).wait_recv()

    @pl.when(me != LAST)
    def _():
        q_direct(LAST).wait_recv()

    for dest in range(STEPS):

        @pl.when(me != dest)
        def _():
            kv_copy(dest, dest).wait_send()

    @pl.when(has_next)
    def _():
        halo.wait_send()

    @pl.when(me == LAST)
    def _():
        for dest in range(LAST):
            q_direct(dest).wait_send()

    @pl.when(me == RELAY)
    def _():
        for dest in RELAYED:
            q_from_relay(dest).wait_send()

    @pl.when(between)
    def _():
        for slot in range(2):
            second_leg(slot).wait_send()

    @pl.when(on_side & (x_lo == 0))
    def _():
        side_second().wait_send()


def finish(out, kvr, qr, win_hbm, dep_hbm, dout, sem):
    window = pltpu.make_async_copy(out, win_hbm, sem.at[0])
    window.start()

    def half(c):
        cols = slice(c * GROUP * HD, (c + 1) * GROUP * HD)
        return pltpu.make_async_copy(dout.at[:, cols], dep_hbm.at[:, cols], sem.at[1 + c])

    token = lax.broadcasted_iota(jnp.int32, (OWN, STEPS * OWN), 0)
    other = lax.broadcasted_iota(jnp.int32, (OWN, STEPS * OWN), 1) % OWN
    for c in range(HK):
        rows = jnp.concatenate(
            [qr[:, h * HD : (h + 1) * HD] for h in range(c * GROUP, (c + 1) * GROUP)], axis=0
        )
        keys = kvr[:, :, c * HD : (c + 1) * HD].reshape(STEPS * OWN, HD)
        values = kvr[:, :, KW + c * HD : KW + (c + 1) * HD].reshape(STEPS * OWN, HD)
        scores = score(rows, keys).reshape(GROUP, OWN, STEPS * OWN)
        scores = jnp.where((token == other)[None], scores, -jnp.inf)
        res = softmax_values(scores.reshape(GROUP * OWN, STEPS * OWN), values).astype(BF16)
        for g in range(GROUP):
            h = c * GROUP + g
            dout[:, h * HD : (h + 1) * HD] = res[g * OWN : (g + 1) * OWN]
        half(c).start()

    window.wait()
    for c in range(HK):
        half(c).wait()


def body(states, w_query, w_key, w_value):
    any_spec = pl.BlockSpec(memory_space=pltpu.HBM)
    dma = pltpu.SemaphoreType.DMA
    args = [
        pltpu.with_memory_space_constraint(a, pltpu.HBM)
        for a in (states[0], w_query, w_key, w_value)
    ]
    vmem = pl.BlockSpec(memory_space=pltpu.VMEM)
    local = pl.pallas_call(
        kernel,
        out_shape=(
            jax.ShapeDtypeStruct((TOK, QW), BF16),
            jax.ShapeDtypeStruct((STEPS, OWN, 2 * KW), BF16),
            jax.ShapeDtypeStruct((OWN, QW), BF16),
        ),
        in_specs=[any_spec] * 4,
        out_specs=(vmem, vmem, vmem),
        scratch_shapes=[
            pltpu.VMEM((TOK, D), BF16),
            pltpu.VMEM((D, QW), BF16),
            pltpu.VMEM((D, 2 * KW), BF16),
            pltpu.VMEM((TOK, QW), BF16),
            pltpu.VMEM((WINDOW + TOK, 2 * KW), BF16),
            pltpu.VMEM((RELAY, OWN, QW), BF16),
            pltpu.VMEM((2, OWN, 2 * KW), BF16),
            pltpu.VMEM((3, BQ, KEYS), F32),
            dma((7,)),
            dma((STEPS,)),
            dma((STEPS,)),
            dma((2,)),
            dma((2,)),
            dma((STEPS,)),
            dma(()),
            dma((RELAY,)),
            dma(()),
            dma(()),
        ],
        compiler_params=pltpu.CompilerParams(
            collective_id=0, has_side_effects=True, vmem_limit_bytes=40 * 1024 * 1024
        ),
        name="looped_attention",
    )(*args)
    window_out, depth_out = pl.pallas_call(
        finish,
        out_shape=(
            jax.ShapeDtypeStruct((TOK, QW), BF16),
            jax.ShapeDtypeStruct((OWN, QW), BF16),
        ),
        in_specs=[vmem] * 3,
        out_specs=(any_spec, any_spec),
        scratch_shapes=[pltpu.VMEM((OWN, QW), BF16), dma((3,))],
        compiler_params=pltpu.CompilerParams(vmem_limit_bytes=16 * 1024 * 1024),
        name="final_attention",
    )(*local)
    return (window_out[None], depth_out)


def solution(mesh):
    in_specs = (P("depth", "tok", None), P(), P(), P())
    out_specs = (P("depth", "tok", None), P(("tok", "depth"), None))
    return jax.shard_map(body, mesh=mesh, in_specs=in_specs, out_specs=out_specs, check_vma=False)
```
